32 devices in a mesh: rep: 2 (over y), ctx: 4 (over z), head: 2 (over x), sub: 2 (over core).
Axes of the slice: x: 2, y: 2, z: 4, core: 2. Of those that a mesh axis runs over, the one named last changes fastest.
Arguments:
- hidden_states: bfloat16 [2048, 4096], P(('rep', 'ctx'), ('head', 'sub')), parts along dimension 0, may hold values from -8 to 8
- w_query: bfloat16 [4096, 2048], P('ctx', ('head', 'sub')), may hold values from -0.09375 to 0.09375
- w_key: bfloat16 [4096, 2048], P('ctx', ('head', 'sub')), may hold values from -0.09375 to 0.09375
- w_value: bfloat16 [4096, 2048], P('ctx', ('head', 'sub')), may hold values from -0.09375 to 0.09375
- a_query: bfloat16 [4096, 8], replicated, may hold values from -0.09375 to 0.09375
- a_value: bfloat16 [4096, 8], replicated, may hold values from -0.09375 to 0.09375
- b_query: bfloat16 [8, 2048], P(None, ('head', 'sub')), may hold values from -0.29882812 to 0.29882812
- b_value: bfloat16 [8, 2048], P(None, ('head', 'sub')), may hold values from -0.29882812 to 0.29882812
- positions: int32 [2048], P(('rep', 'ctx')), parts along dimension 0, may hold values from 0 to 99999, as said below
- out_grad: bfloat16 [2048, 2048], P(('rep', 'ctx'), ('head', 'sub')), parts along dimension 0, may hold values from -0.119628906 to 0.119628906
Outputs:
- attn_out: bfloat16 [2048, 2048], P(('rep', 'ctx'), ('head', 'sub')), parts along dimension 0
- grad_a_query: float32 [4096, 16], P(None, 'rep'), parts along dimension 1
- grad_b_query: float32 [16, 2048], P('rep', ('head', 'sub')), parts along dimension 0
- grad_a_value: float32 [4096, 16], P(None, 'rep'), parts along dimension 1
- grad_b_value: float32 [16, 2048], P('rep', ('head', 'sub')), parts along dimension 0
The draws below stay inside these ranges and needn't reach their ends.
There are 2 independent parts, one for each index of `rep`. The reference program is written for one: setup_inputs(seed, part) draws one part's arguments, and reference() takes and returns one part's arrays. A program takes and returns all parts, laid end to end along the dimension named above; an argument that names none is the same for every part. Nothing has to cross between parts.
Inputs may be any that keep to these rules, and one draw needn't show every extreme that they name: `positions`: strictly increasing along the sequence; the first is 0 and the last is 99999.
All inputs are finite; a program needn't handle non-finite values.
Results may differ from the reference program's by a relative error of at most 0.012.
Values may be sent and summed in bfloat16 or wider, within the bound.
A program may use at most 64 MiB of HBM per device.

```python
import math
import jax
import jax.numpy as jnp
from jax import lax

D = 4096
HEAD_DIM = 128
HEADS = 16
RANK = 8
TRAIN_CTX = 4096
MAX_POS = 100000
HD = 2048
TOKENS = 1024
GROUP = 256


def draw_hidden_states(key, part):
    normal_key = jax.random.fold_in(jax.random.fold_in(key, 11), 0)
    entries = jnp.clip(jax.random.normal(normal_key, (TOKENS, D), jnp.float32), -4.0, 4.0)
    return entries.astype(jnp.bfloat16)


def draw_positions(key, part):
    cut_key, split_key = jax.random.split(jax.random.fold_in(key, 23))
    cuts = jnp.sort(jax.random.randint(cut_key, (3,), 1, TOKENS))
    extra = MAX_POS - TOKENS
    splits = jnp.sort(jax.random.randint(split_key, (2,), 0, extra + 1))
    jumps = jnp.stack([splits[0], splits[1] - splits[0], extra - splits[1]])
    steps_along = jnp.arange(TOKENS, dtype=jnp.int32)
    skipped = jnp.sum(jnp.where(steps_along[:, None] >= cuts[None, :], jumps[None, :], 0), axis=1)
    return (steps_along + skipped).astype(jnp.int32)


def levels(key, shape, shards, least, largest):
    loudness, own = 1.0, jax.random.fold_in(key, 6)
    for axis_at, shards_of in shards:
        draws = jnp.exp(jax.random.uniform(jax.random.fold_in(own, axis_at), (shards_of,), jnp.float32, least / len(shards), largest / len(shards)))
        loudness = loudness * jnp.repeat(draws, shape[axis_at] // shards_of).reshape([-1 if axis == axis_at else 1 for axis in range(len(shape))])
    return loudness


def gaussian(rng, extent, deviation, reach, shards=(), held_as=jnp.bfloat16):
    drawn = jax.random.normal(rng, extent, jnp.float32) * deviation
    if len(shards) > 0:
        drawn = levels(rng, extent, shards, -0.22, 0.18) * drawn
    return jnp.clip(drawn, min=-reach, max=reach).astype(held_as)


def setup_inputs(seed: int = 0, part: int = 0) -> dict:
    streams_of = jax.random.split(jax.random.key(seed), 11)
    part_keys = jax.random.split(jax.random.fold_in(streams_of[10], part), 11)
    hidden_states = draw_hidden_states(jax.random.fold_in(jax.random.fold_in(streams_of[10], part), 71), part)
    w_query = gaussian(streams_of[1], (D, HD), D ** -0.5, 0.09375, ((0, 4), (1, 4)))
    w_key = gaussian(streams_of[2], (D, HD), D ** -0.5, 0.09375, ((0, 4), (1, 4)))
    w_value = gaussian(streams_of[3], (D, HD), D ** -0.5, 0.09375, ((0, 4), (1, 4)))
    a_query = gaussian(streams_of[4], (D, RANK), D ** -0.5, 0.09375)
    a_value = gaussian(streams_of[5], (D, RANK), D ** -0.5, 0.09375)
    b_query = gaussian(streams_of[6], (RANK, HD), 0.05, 0.29882812, ((1, 4),))
    b_value = gaussian(streams_of[7], (RANK, HD), 0.05, 0.29882812, ((1, 4),))
    positions = draw_positions(jax.random.fold_in(jax.random.fold_in(streams_of[10], part), 71), part)
    out_grad = gaussian(part_keys[9], (TOKENS, HD), 0.02, 0.119628906, ((0, 4), (1, 4)))
    return {"hidden_states": hidden_states, "w_query": w_query, "w_key": w_key, "w_value": w_value, "a_query": a_query, "a_value": a_value, "b_query": b_query, "b_value": b_value, "positions": positions, "out_grad": out_grad}


def rope_tables(positions):
    half_dim = HEAD_DIM // 2
    inverse = jnp.exp(jnp.arange(half_dim, dtype=jnp.float32) * (-2.0 * math.log(10000.0) / HEAD_DIM))
    scaled = positions.astype(jnp.float32) * (TRAIN_CTX / MAX_POS)
    angle = scaled[:, None] * inverse[None, :]
    return (jnp.cos(angle)[:, None, :], jnp.sin(angle)[:, None, :])

def rotate(vectors, cosine, sine):
    half_dim = vectors.shape[-1] // 2
    first = vectors[..., :half_dim]
    second = vectors[..., half_dim:]
    return jnp.concatenate([first * cosine - second * sine, second * cosine + first * sine], axis=-1)

def head_pass(operands):
    queries, keys, values, grads, moved = operands
    amount = moved * (GROUP // 2)
    groups = TOKENS // GROUP
    scale = 1.0 / math.sqrt(HEAD_DIM)

    def arrange(tensor):
        return jnp.roll(tensor, -amount, axis=0).reshape(groups, GROUP, HEAD_DIM).astype(jnp.float32)
    query_f, key_f, value_f, grad_f = (arrange(queries), arrange(keys), arrange(values), arrange(grads))
    allowed = jnp.arange(GROUP)[:, None] >= jnp.arange(GROUP)[None, :]
    scores = jnp.einsum('gqd,gkd->gqk', query_f, key_f) * scale
    scores = jnp.where(allowed, scores, -jnp.inf)
    highest = lax.optimization_barrier(jnp.max(scores, axis=-1, keepdims=True))
    expo = jnp.where(allowed, jnp.exp(scores - highest), 0.0)
    probs = expo / lax.optimization_barrier(jnp.sum(expo, axis=-1, keepdims=True))
    probs_b = lax.optimization_barrier(probs.astype(jnp.bfloat16)).astype(jnp.float32)
    output = jnp.einsum('gqk,gkd->gqd', probs_b, value_f)
    output_b = lax.optimization_barrier(output.astype(jnp.bfloat16)).astype(jnp.float32)
    dprob = jnp.einsum('gqd,gkd->gqk', grad_f, value_f)
    delta = lax.optimization_barrier(jnp.sum(grad_f * output_b, axis=-1, keepdims=True))
    dscore = probs * (dprob - delta)
    dscore_b = lax.optimization_barrier((dscore * scale).astype(jnp.bfloat16)).astype(jnp.float32)
    dquery = jnp.einsum('gqk,gkd->gqd', dscore_b, key_f)
    dvalue = jnp.einsum('gqk,gqd->gkd', probs_b, grad_f)

    def restore(tensor):
        return jnp.roll(tensor.reshape(TOKENS, HEAD_DIM), amount, axis=0)
    return (restore(output_b).astype(jnp.bfloat16), restore(dquery), restore(dvalue))

def reference(hidden_states, w_query, w_key, w_value, a_query, a_value, b_query, b_value, positions, out_grad):
    cosine, sine = rope_tables(positions)
    base_q = jnp.dot(hidden_states, w_query, preferred_element_type=jnp.float32)
    base_k = jnp.dot(hidden_states, w_key, preferred_element_type=jnp.float32)
    base_v = jnp.dot(hidden_states, w_value, preferred_element_type=jnp.float32)
    low_q = jnp.dot(hidden_states, a_query, preferred_element_type=jnp.float32).astype(jnp.bfloat16)
    low_v = jnp.dot(hidden_states, a_value, preferred_element_type=jnp.float32).astype(jnp.bfloat16)
    pre_q = base_q + 2.0 * jnp.dot(low_q, b_query, preferred_element_type=jnp.float32)
    queries = rotate(pre_q.reshape(TOKENS, HEADS, HEAD_DIM), cosine, sine).astype(jnp.bfloat16)
    keys = rotate(base_k.reshape(TOKENS, HEADS, HEAD_DIM), cosine, sine).astype(jnp.bfloat16)
    values = (base_v + 2.0 * jnp.dot(low_v, b_value, preferred_element_type=jnp.float32)).astype(jnp.bfloat16)
    values = values.reshape(TOKENS, HEADS, HEAD_DIM)
    grads = out_grad.reshape(TOKENS, HEADS, HEAD_DIM)
    moved = (jnp.arange(HEADS) >= HEADS // 2).astype(jnp.int32)
    outputs, dquery, dvalue = lax.map(head_pass, (queries.transpose(1, 0, 2), keys.transpose(1, 0, 2), values.transpose(1, 0, 2), grads.transpose(1, 0, 2), moved))
    attn_out = outputs.transpose(1, 0, 2).reshape(TOKENS, HD)
    dq = rotate(dquery.transpose(1, 0, 2), cosine, -sine).astype(jnp.bfloat16).reshape(TOKENS, HD)
    dv = dvalue.transpose(1, 0, 2).astype(jnp.bfloat16).reshape(TOKENS, HD)
    grad_b_query = 2.0 * jnp.dot(low_q.T, dq, preferred_element_type=jnp.float32)
    grad_b_value = 2.0 * jnp.dot(low_v.T, dv, preferred_element_type=jnp.float32)
    low_grads = jnp.concatenate([2.0 * jnp.dot(dq, b_query.T, preferred_element_type=jnp.float32), 2.0 * jnp.dot(dv, b_value.T, preferred_element_type=jnp.float32)], axis=1)
    grad_down = lax.dot_general(hidden_states.astype(jnp.float32), low_grads, (((0,), (0,)), ((), ())), precision=lax.Precision.HIGHEST)
    return (attn_out, grad_down[:, :RANK], grad_b_query, grad_down[:, RANK:], grad_b_value)
```

```python
import functools
import math

import jax
import jax.numpy as jnp
from jax import lax
from jax.experimental import pallas as pl
from jax.experimental.pallas import tpu as pltpu
from jax.sharding import PartitionSpec as P

HEAD_DIM = 128
HEADS = 16
TRAIN_CTX = 4096
MAX_POS = 100000


def passed_along(block, axis, distance):
    devices = range(lax.axis_size(axis))
    route = [((i - distance) % len(devices), i) for i in devices]
    return lax.ppermute(block, axis, route)


def rope_tables(positions):
    half_dim = HEAD_DIM // 2
    inverse = jnp.exp(
        jnp.arange(half_dim, dtype=jnp.float32) * (-2.0 * math.log(10000.0) / HEAD_DIM)
    )
    scaled = positions.astype(jnp.float32) * (TRAIN_CTX / MAX_POS)
    angle = scaled[:, None] * inverse[None, :]
    return (jnp.cos(angle)[:, None, :], jnp.sin(angle)[:, None, :])


def rotate(vectors, cosine, sine):
    half_dim = vectors.shape[-1] // 2
    first = vectors[..., :half_dim]
    second = vectors[..., half_dim:]
    return jnp.concatenate(
        [first * cosine - second * sine, second * cosine + first * sine], axis=-1
    )


def project_back(features, low_grads):
    block_width = min(features.shape[1], 512)
    block_count = features.shape[1] // block_width

    def one_block(number):
        section = lax.dynamic_slice_in_dim(features, number * block_width, block_width, 1).astype(
            jnp.float32
        )
        return lax.dot_general(
            section, low_grads, (((0,), (0,)), ((), ())), precision=lax.Precision.HIGHEST
        )

    blocks = lax.map(one_block, jnp.arange(block_count))
    return blocks.reshape(features.shape[1], low_grads.shape[1])


def local(
    hidden_states, w_query, w_key, w_value, a_query, a_value, b_query, b_value, positions, out_grad
):
    rows_here = hidden_states.shape[0]
    columns = w_query.shape[1]
    heads_here = columns // HEAD_DIM
    rank_cols = a_query.shape[1]
    scale = 1.0 / math.sqrt(HEAD_DIM)
    shard_count = lax.axis_size("ctx")
    total_tokens = rows_here * shard_count
    group_len = total_tokens // 4
    reach = (group_len // 2 % rows_here + group_len - 1) // rows_here
    full_states = lax.all_gather(hidden_states, ("head", "sub"), axis=1, tiled=True)
    pieces = (
        lax.all_gather(w_query, "ctx", axis=0, tiled=True),
        lax.all_gather(w_key, "ctx", axis=0, tiled=True),
        lax.all_gather(w_value, "ctx", axis=0, tiled=True),
    )
    base_q, base_k, base_v = tuple(
        (
            jnp.dot(full_states, weights_piece, preferred_element_type=jnp.float32)
            for weights_piece in pieces
        )
    )
    low_q = jnp.dot(full_states, a_query, preferred_element_type=jnp.float32).astype(jnp.bfloat16)
    low_v = jnp.dot(full_states, a_value, preferred_element_type=jnp.float32).astype(jnp.bfloat16)
    cosine, sine = rope_tables(positions)
    pre_q = base_q + 2.0 * jnp.dot(low_q, b_query, preferred_element_type=jnp.float32)
    queries = rotate(pre_q.reshape(rows_here, heads_here, HEAD_DIM), cosine, sine).astype(
        jnp.bfloat16
    )
    keyed = rotate(base_k.reshape(rows_here, heads_here, HEAD_DIM), cosine, sine).astype(
        jnp.bfloat16
    )
    valued = (base_v + 2.0 * jnp.dot(low_v, b_value, preferred_element_type=jnp.float32)).astype(
        jnp.bfloat16
    )
    valued = valued.reshape(rows_here, heads_here, HEAD_DIM)
    current = jnp.stack([keyed, valued])
    collected = [current]
    for level in range(reach):
        current = passed_along(current, "ctx", 1)
        collected.append(current)
    key_rows = jnp.concatenate([block[0] for block in collected], axis=0)
    value_rows = jnp.concatenate([block[1] for block in collected], axis=0)
    shard_id = lax.axis_index("ctx")
    head_ids = lax.axis_index(("head", "sub")) * heads_here + jnp.arange(heads_here)
    amount = jnp.where(head_ids >= HEADS // 2, group_len // 2, 0).astype(jnp.int32)
    query_pos = shard_id * rows_here + jnp.arange(rows_here, dtype=jnp.int32)
    block_ids = jnp.arange(reach + 1, dtype=jnp.int32)
    source_shard = (shard_id - block_ids) % shard_count
    key_pos = (
        source_shard[:, None] * rows_here + jnp.arange(rows_here, dtype=jnp.int32)[None, :]
    ).reshape(-1)
    query_num = (query_pos[None, :] - amount[:, None]) % total_tokens
    key_num = (key_pos[None, :] - amount[:, None]) % total_tokens
    same_group = key_num[:, None, :] // group_len == query_num[:, :, None] // group_len
    visible = same_group & (key_num[:, None, :] <= query_num[:, :, None])
    scores = (
        jnp.einsum("qhd,khd->hqk", queries, key_rows, preferred_element_type=jnp.float32) * scale
    )
    scores = jnp.where(visible, scores, -jnp.inf)
    highest = jnp.max(scores, axis=-1, keepdims=True)
    expo = jnp.where(visible, jnp.exp(scores - highest), 0.0)
    probs = expo / jnp.sum(expo, axis=-1, keepdims=True)
    probs_b = probs.astype(jnp.bfloat16)
    attended = jnp.einsum("hqk,khd->qhd", probs_b, value_rows, preferred_element_type=jnp.float32)
    attn_out = attended.astype(jnp.bfloat16)
    grads = out_grad.reshape(rows_here, heads_here, HEAD_DIM)
    dprob = jnp.einsum("qhd,khd->hqk", grads, value_rows, preferred_element_type=jnp.float32)
    delta = jnp.sum(grads.astype(jnp.float32) * attn_out.astype(jnp.float32), axis=-1)
    dscore = probs * (dprob - delta.T[:, :, None])
    dscore_b = (dscore * scale).astype(jnp.bfloat16)
    dquery = jnp.einsum("hqk,khd->qhd", dscore_b, key_rows, preferred_element_type=jnp.float32)
    dvalue = jnp.einsum("hqk,qhd->khd", probs_b, grads, preferred_element_type=jnp.float32)
    value_blocks = dvalue.reshape(reach + 1, rows_here, columns)
    carried = value_blocks[reach]
    for level in range(reach, 0, -1):
        carried = passed_along(carried, "ctx", -1) + value_blocks[level - 1]
    dv_local = carried.astype(jnp.bfloat16)
    dq_local = rotate(dquery, cosine, -sine).astype(jnp.bfloat16).reshape(rows_here, columns)
    grad_bq = 2.0 * jnp.dot(low_q.T, dq_local, preferred_element_type=jnp.float32)
    grad_bv = 2.0 * jnp.dot(low_v.T, dv_local, preferred_element_type=jnp.float32)
    low_grads = jnp.concatenate(
        [
            2.0 * jnp.dot(dq_local, b_query.T, preferred_element_type=jnp.float32),
            2.0 * jnp.dot(dv_local, b_value.T, preferred_element_type=jnp.float32),
        ],
        axis=1,
    )
    grad_down = lax.psum(project_back(full_states, low_grads), ("ctx", "head", "sub"))
    grad_bq, grad_bv = lax.psum((grad_bq, grad_bv), "ctx")
    return (
        attn_out.reshape(rows_here, columns),
        grad_down[:, :rank_cols],
        grad_bq,
        grad_down[:, rank_cols:],
        grad_bv,
    )


LANES = 128
MESH = pl.DeviceIdType.MESH


def one_head_kernel(
    n,
    subs,
    wide,
    hid_ref,
    wq_ref,
    wk_ref,
    wv_ref,
    a_ref,
    bq_ref,
    bv_ref,
    pos_ref,
    og_ref,
    inv_ref,
    out_ref,
    gb_ref,
    ga_ref,
    hbuf,
    wbuf,
    ogbuf,
    posbuf,
    ctab,
    stab,
    qbuf,
    kbuf,
    vbuf,
    lowbuf,
    dqbuf,
    dvbuf,
    obuf,
    outbuf,
    gbsend,
    gbrecv,
    rsend,
    rrecv,
    total,
    agbuf,
    local_sem,
    hz_send,
    hx_send,
    hs_send,
    h_recv,
    w_send,
    wy_send,
    w_recv,
    og_send,
    og_recv,
    pos_send,
    pos_recv,
    out_send,
    out_recv,
    gb_send,
    gb_recv,
    rs_send,
    rs_recv,
    ag_send,
    ag_recv,
):
    f32, bf16 = jnp.float32, jnp.bfloat16
    rows, width = hid_ref.shape
    depth = wq_ref.shape[0]
    half = depth // 2
    tokens = rows * n
    group = tokens // 4
    r, c = lax.axis_index("rep"), lax.axis_index("ctx")
    h, s = lax.axis_index("head"), lax.axis_index("sub")
    hs = h * subs + s
    members = n * wide
    me = c * wide + hs
    weights = (wq_ref, wk_ref, wv_ref)
    pending = []

    def member(number):
        col = lax.rem(number, wide)
        return {"ctx": number // wide, "head": col // subs, "sub": lax.rem(col, subs)}

    def remote(src, dst, send, recv, device):
        return pltpu.make_async_remote_copy(
            src_ref=src, dst_ref=dst, send_sem=send, recv_sem=recv, device_id=device, device_id_type=MESH
        )

    def launch(copy, cond=None):
        if cond is None:
            copy.start()
        else:
            pl.when(cond)(copy.start)
        pending.append((copy, cond))

    barrier = pltpu.get_barrier_semaphore()
    for k in range(1, members):
        pl.semaphore_signal(
            barrier, inc=1, device_id=member(lax.rem(me + k, members)), device_id_type=MESH
        )
    pl.semaphore_signal(barrier, inc=1, device_id={"rep": 1 - r}, device_id_type=MESH)

    def cols(number, size):
        return pl.ds(pl.multiple_of(number * size, LANES), size)

    def part(number, size):
        return pl.ds(pl.multiple_of(number * size, 8), size)

    def hblk(block, column):
        return hbuf.at[part(block, rows), cols(column, width)]

    def wblk(block, which, side):
        return wbuf.at[
            pl.ds(pl.multiple_of(block * depth + side * half, 8), half), pl.ds(which * LANES, LANES)
        ]

    locals_ = [
        pltpu.make_async_copy(hid_ref, hblk(c, hs), local_sem.at[0]),
        pltpu.make_async_copy(a_ref, wbuf.at[:, pl.ds(3 * LANES, LANES)], local_sem.at[1]),
        pltpu.make_async_copy(og_ref.at[:, cols(c, LANES)], ogbuf.at[part(c, rows), :], local_sem.at[2]),
        pltpu.make_async_copy(pos_ref, posbuf.at[c], local_sem.at[3]),
    ]
    for m in range(3):
        locals_.append(
            pltpu.make_async_copy(
                weights[m].at[:, cols(c, LANES)],
                wbuf.at[part(c, depth), pl.ds(m * LANES, LANES)],
                local_sem.at[4 + m],
            )
        )
    for copy in locals_:
        copy.start()
    pl.semaphore_wait(barrier, members)

    def spread(src, block):
        launch(
            remote(src, hblk(block, hs), hx_send.at[block], h_recv.at[block, hs], {"head": 1 - h})
        )
        launch(
            remote(src, hblk(block, hs), hs_send.at[0, block], h_recv.at[block, hs], {"sub": 1 - s})
        )

    def arrived(block, column):
        return remote(
            hblk(block, column), hblk(block, column), hx_send.at[0], h_recv.at[block, column], {"sub": 1 - s}
        )

    def go_up(src, block):
        return remote(src, hblk(block, hs), hz_send.at[0, block], h_recv.at[block, hs], {"ctx": c + 1})

    def go_down(src, block):
        return remote(src, hblk(block, hs), hz_send.at[1, block], h_recv.at[block, hs], {"ctx": c - 1})

    def send_w(t, sign):
        target = c + sign * t
        cond = (target < n) if sign > 0 else (target >= 0)
        slot = 2 * (t - 1) + (1 if sign > 0 else 0)
        for m in range(3):
            launch(
                remote(
                    weights[m].at[pl.ds(pl.multiple_of(r * half, 8), half), cols(target, LANES)],
                    wblk(c, m, r),
                    w_send.at[slot, m],
                    w_recv.at[c, m, r],
                    {"ctx": target},
                ),
                cond,
            )

    def pass_w(block, cond):
        for m in range(3):
            copy = remote(
                wblk(block, m, r), wblk(block, m, r), wy_send.at[block, m], w_recv.at[block, m, r], {"rep": 1 - r}
            )

            @pl.when(cond)
            def _():
                copy.wait_recv()
                copy.start()

            pending.append((copy, cond))

    def pass_x(block, cond):
        copy = remote(
            hblk(block, (1 - h) * subs + s),
            hblk(block, (1 - h) * subs + s),
            hs_send.at[1, block],
            h_recv.at[block, (1 - h) * subs + s],
            {"sub": 1 - s},
        )

        def act():
            copy.wait_recv()
            copy.start()

        if cond is None:
            act()
        else:
            pl.when(cond)(act)
        pending.append((copy, cond))

    launch(go_up(hid_ref, c), c < n - 1)
    launch(go_down(hid_ref, c), c > 0)
    spread(hid_ref, c)
    for t in range(1, n):
        for sign in (1, -1):
            target = c + sign * t
            cond = (target < n) if sign > 0 else (target >= 0)
            slot = 2 * (t - 1) + (1 if sign > 0 else 0)
            launch(
                remote(pos_ref, posbuf.at[c], pos_send.at[slot], pos_recv.at[c], {"ctx": target}), cond
            )
            launch(
                remote(
                    og_ref.at[:, cols(target, LANES)],
                    ogbuf.at[part(c, rows), :],
                    og_send.at[slot],
                    og_recv.at[c],
                    {"ctx": target},
                ),
                cond,
            )
    send_w(1, 1)
    send_w(1, -1)
    pass_x(c, None)

    def hidden_step(t):
        low_block, high_block = c - t, c + t

        @pl.when(low_block >= 0)
        def _():
            arrived(low_block, hs).wait_recv()

        for copy_of, block, cond, more in (
            (go_up, low_block, low_block >= 0, c < n - 1),
            (go_down, high_block, high_block < n, c > 0),
        ):
            if copy_of is go_down:

                @pl.when(cond)
                def _():
                    arrived(high_block, hs).wait_recv()

            launch(copy_of(hblk(block, hs), block), cond & more)
            for copy in (
                remote(hblk(block, hs), hblk(block, hs), hx_send.at[block], h_recv.at[block, hs], {"head": 1 - h}),
                remote(hblk(block, hs), hblk(block, hs), hs_send.at[0, block], h_recv.at[block, hs], {"sub": 1 - s}),
            ):
                launch(copy, cond)

    def x_step(t):
        pass_x(c - t, c - t >= 0)
        pass_x(c + t, c + t < n)

    def w_step(t):
        pass_w(c - t, c - t >= 0)
        pass_w(c + t, c + t < n)

    def tables():
        for block in range(n):

            @pl.when(block != c)
            def _():
                remote(pos_ref, posbuf.at[block], pos_send.at[0], pos_recv.at[block], {"sub": 1 - s}).wait_recv()

        locals_[3].wait()
        lane = lax.broadcasted_iota(jnp.int32, (LANES, LANES), 1)
        chunks = rows // LANES

        def one(number, carry):
            row = posbuf[number // chunks, pl.ds(lax.rem(number, chunks), 1), :].astype(f32)
            column = jnp.transpose(jnp.broadcast_to(row, (LANES, LANES)))
            angle = (column * (TRAIN_CTX / MAX_POS)) * inv_ref[0:1, :]
            here = part(number, LANES)
            ctab[here, :] = jnp.cos(angle)
            sine = jnp.sin(angle)
            stab[here, :] = jnp.where(lane < LANES // 2, -sine, sine)
            return carry

        lax.fori_loop(0, tokens // LANES, one, 0)

    for t in range(1, n):
        hidden_step(t)
        if t + 1 < n:
            send_w(t + 1, 1)
            send_w(t + 1, -1)
        if t == 1:
            tables()
        x_step(t)
        if t > 1:
            w_step(t - 1)
    w_step(n - 1)

    for block in range(n):
        for column in range(wide):
            mine = (column // subs == h) & (column % subs == s)
            across = (column // subs != h) & (column % subs == s)

            @pl.when(jnp.logical_not(mine | across))
            def _():
                arrived(block, column).wait_recv()

        @pl.when(block != c)
        def _():
            for m in range(3):
                remote(
                    wblk(block, m, 1 - r), wblk(block, m, 1 - r), wy_send.at[0, 0], w_recv.at[block, m, 1 - r], {"rep": 1 - r}
                ).wait_recv()
            remote(
                ogbuf.at[part(block, rows), :], ogbuf.at[part(block, rows), :], og_send.at[0], og_recv.at[block], {"sub": 1 - s}
            ).wait_recv()

    for number, copy in enumerate(locals_):
        if number != 3:
            copy.wait()

    def turn(u, cosine, sine):
        return u * cosine + pltpu.roll(u, LANES // 2, 1) * sine

    def project(block, carry):
        here = part(block, rows)
        y = jnp.dot(hbuf[here, :], wbuf[...], preferred_element_type=f32)
        low = y[:, 3 * LANES :].astype(bf16)
        lowbuf[here, :] = low
        cosine, sine = ctab[here, :], stab[here, :]
        pre_q = y[:, :LANES] + 2.0 * jnp.dot(low, bq_ref[...], preferred_element_type=f32)
        qbuf[here, :] = turn(pre_q, cosine, sine).astype(bf16)
        kbuf[here, :] = turn(y[:, LANES : 2 * LANES], cosine, sine).astype(bf16)
        vbuf[here, :] = (
            y[:, 2 * LANES : 3 * LANES] + 2.0 * jnp.dot(low, bv_ref[...], preferred_element_type=f32)
        ).astype(bf16)
        return carry

    lax.fori_loop(0, n, project, 0)

    shift = jnp.where(hs * n + c >= HEADS // 2, group // 2, 0)
    scale = 1.0 / math.sqrt(HEAD_DIM)
    hg = group // 2
    dot_t = functools.partial(
        lax.dot_general, dimension_numbers=(((1,), (1,)), ((), ())), preferred_element_type=f32
    )
    t_dot = functools.partial(
        lax.dot_general, dimension_numbers=(((0,), (0,)), ((), ())), preferred_element_type=f32
    )
    allowed = lax.broadcasted_iota(jnp.int32, (group, group), 0) >= lax.broadcasted_iota(
        jnp.int32, (group, group), 1
    )

    def attend(g, carry):
        first = pl.ds(pl.multiple_of(lax.rem(g * group + shift, tokens), 8), hg)
        second = pl.ds(pl.multiple_of(lax.rem(g * group + hg + shift, tokens), 8), hg)

        def take(ref):
            return jnp.concatenate([ref[first, :], ref[second, :]], axis=0)

        def put(ref, value):
            ref[first, :] = value[:hg]
            ref[second, :] = value[hg:]

        q, k, v, grad = take(qbuf), take(kbuf), take(vbuf), take(ogbuf)
        scores = jnp.where(allowed, dot_t(q, k) * scale, -jnp.inf)
        highest = jnp.max(scores, axis=-1, keepdims=True)
        expo = jnp.where(allowed, jnp.exp(scores - highest), 0.0)
        probs = expo / jnp.sum(expo, axis=-1, keepdims=True)
        probs_b = probs.astype(bf16)
        out = jnp.dot(probs_b, v, preferred_element_type=f32).astype(bf16)
        put(obuf, out)
        dprob = dot_t(grad, v)
        delta = jnp.sum(grad.astype(f32) * out.astype(f32), axis=-1, keepdims=True)
        dscore_b = (probs * (dprob - delta) * scale).astype(bf16)
        dq = jnp.dot(dscore_b, k, preferred_element_type=f32)
        put(dqbuf, turn(dq, take(ctab), -take(stab)).astype(bf16))
        put(dvbuf, t_dot(probs_b, grad).astype(bf16))
        return carry

    lax.fori_loop(0, tokens // group, attend, 0)

    dq, dv, low = dqbuf[...], dvbuf[...], lowbuf[...]
    low_t = 2.0 * (dot_t(bq_ref[0:16, :], dq) + dot_t(bv_ref[0:16, :], dv))
    for k in range(members):
        at = (k // 2) * LANES
        rsend[k] = low_t[8 * (k % 2) : 8 * (k % 2) + 8, at : at + LANES]
    for k in range(1, members):
        to = lax.rem(me + k, members)
        launch(remote(rsend.at[to], rrecv.at[me], rs_send.at[k], rs_recv.at[me], member(to)))
    for t in range(1, n):
        for sign in (1, -1):
            target = c + sign * t
            cond = (target < n) if sign > 0 else (target >= 0)
            slot = 2 * (t - 1) + (1 if sign > 0 else 0)
            launch(
                remote(
                    obuf.at[part(target, rows), :], outbuf.at[c], out_send.at[slot], out_recv.at[c], {"ctx": target}
                ),
                cond,
            )
    gbsend[0:8, :] = (2.0 * t_dot(low, dq))[0:8]
    gbsend[8:16, :] = (2.0 * t_dot(low, dv))[8:16]
    out_ref[:, cols(c, LANES)] = obuf[part(c, rows), :]
    gb_ref[:, cols(c, LANES)] = gbsend[...]

    rrecv[me] = rsend[me]
    for k in range(1, members):
        frm = lax.rem(me + k, members)
        remote(rsend.at[0], rrecv.at[frm], rs_send.at[0], rs_recv.at[frm], {"sub": 1 - s}).wait_recv()
    reduced = rrecv[0]
    for k in range(1, members):
        reduced = reduced + rrecv[k]
    total[...] = reduced
    agbuf[me] = reduced
    for k in range(1, members):
        to = lax.rem(me + k, members)
        launch(remote(total, agbuf.at[me], ag_send.at[k], ag_recv.at[me], member(to)))
    for t in range(1, n):
        for sign in (1, -1):
            target = c + sign * t
            cond = (target < n) if sign > 0 else (target >= 0)
            slot = 2 * (t - 1) + (1 if sign > 0 else 0)
            launch(
                remote(gbsend, gbrecv.at[c], gb_send.at[slot], gb_recv.at[c], {"ctx": target}), cond
            )
    for block in range(n):

        @pl.when(block != c)
        def _():
            remote(gbsend, gbrecv.at[block], gb_send.at[0], gb_recv.at[block], {"sub": 1 - s}).wait_recv()
            remote(outbuf.at[block], outbuf.at[block], out_send.at[0], out_recv.at[block], {"sub": 1 - s}).wait_recv()
            gb_ref[:, block * LANES : (block + 1) * LANES] = gbrecv[block]
            out_ref[:, block * LANES : (block + 1) * LANES] = outbuf[block]

    for k in range(1, members):
        frm = lax.rem(me + k, members)
        remote(total, agbuf.at[frm], ag_send.at[0], ag_recv.at[frm], {"sub": 1 - s}).wait_recv()
    full = jnp.concatenate(
        [
            jnp.concatenate([agbuf[2 * k + side] for k in range(members // 2)], axis=1)
            for side in range(2)
        ],
        axis=0,
    )
    upper = full.astype(bf16)
    lower = (full - upper.astype(f32)).astype(bf16)
    both = jnp.concatenate([upper, lower], axis=0)
    tile = 512

    def back(number, carry):
        here = pl.ds(pl.multiple_of(number * tile, LANES), tile)
        product = jnp.dot(both, hbuf[:, here], preferred_element_type=f32)
        ga_ref[:, here] = product[0:16] + product[16:32]
        return carry

    lax.fori_loop(0, hbuf.shape[1] // tile, back, 0)
    for copy, cond in pending:
        if cond is None:
            copy.wait_send()
        else:
            pl.when(cond)(copy.wait_send)


def one_head(
    hidden_states, w_query, w_key, w_value, a_query, a_value, b_query, b_value, positions, out_grad
):
    f32, bf16 = jnp.float32, jnp.bfloat16
    n, subs = lax.axis_size("ctx"), lax.axis_size("sub")
    wide = subs * lax.axis_size("head")
    rows, width = hidden_states.shape
    model = a_query.shape[0]
    rank = a_query.shape[1]
    tokens = rows * n
    columns = w_query.shape[1]
    members = n * wide
    c = lax.axis_index("ctx")
    a_pad = jnp.pad(jnp.concatenate([a_query, a_value], axis=1), ((0, 0), (0, LANES - 2 * rank)))
    bq = lax.dynamic_slice_in_dim(b_query, c * LANES, LANES, 1)
    bv = lax.dynamic_slice_in_dim(b_value, c * LANES, LANES, 1)
    bq = jnp.pad(bq, ((0, LANES - rank), (0, 0)))
    bv = jnp.pad(bv, ((rank, LANES - 2 * rank), (0, 0)))
    half_dim = HEAD_DIM // 2
    inverse = jnp.exp(
        jnp.arange(half_dim, dtype=f32) * (-2.0 * math.log(10000.0) / HEAD_DIM)
    )
    inverse = jnp.broadcast_to(jnp.concatenate([inverse, inverse])[None, :], (8, LANES))
    pos = positions.reshape(rows // LANES, LANES)
    pos = jnp.pad(pos, ((0, 8 - rows // LANES), (0, 0)))
    vmem, dma = pltpu.VMEM, pltpu.SemaphoreType.DMA
    hbm_spec = pl.BlockSpec(memory_space=pl.ANY)
    vmem_spec = pl.BlockSpec(memory_space=pltpu.VMEM)
    out, gb, ga = pl.pallas_call(
        functools.partial(one_head_kernel, n, subs, wide),
        out_shape=(
            jax.ShapeDtypeStruct((rows, columns), bf16),
            jax.ShapeDtypeStruct((2 * rank, columns), f32),
            jax.ShapeDtypeStruct((2 * rank, model), f32),
        ),
        in_specs=[hbm_spec] * 5 + [vmem_spec] * 2 + [hbm_spec] * 2 + [vmem_spec],
        out_specs=[vmem_spec] * 3,
        scratch_shapes=[
            vmem((tokens, model), bf16),
            vmem((model, 4 * LANES), bf16),
            vmem((tokens, LANES), bf16),
            vmem((n, 8, LANES), jnp.int32),
            vmem((tokens, LANES), f32),
            vmem((tokens, LANES), f32),
            vmem((tokens, LANES), bf16),
            vmem((tokens, LANES), bf16),
            vmem((tokens, LANES), bf16),
            vmem((tokens, LANES), bf16),
            vmem((tokens, LANES), bf16),
            vmem((tokens, LANES), bf16),
            vmem((tokens, LANES), bf16),
            vmem((n, rows, LANES), bf16),
            vmem((2 * rank, LANES), f32),
            vmem((n, 2 * rank, LANES), f32),
            vmem((members, 8, LANES), f32),
            vmem((members, 8, LANES), f32),
            vmem((8, LANES), f32),
            vmem((members, 8, LANES), f32),
            dma((7,)),
            dma((2, n)),
            dma((n,)),
            dma((2, n)),
            dma((n, wide)),
            dma((2 * n, 3)),
            dma((n, 3)),
            dma((n, 3, 2)),
            dma((2 * n,)),
            dma((n,)),
            dma((2 * n,)),
            dma((n,)),
            dma((2 * n,)),
            dma((n,)),
            dma((2 * n,)),
            dma((n,)),
            dma((members,)),
            dma((members,)),
            dma((members,)),
            dma((members,)),
        ],
        compiler_params=pltpu.CompilerParams(
            collective_id=0, has_side_effects=True, vmem_limit_bytes=56 * 1024 * 1024
        ),
    )(hidden_states, w_query, w_key, w_value, a_pad, bq, bv, pos, out_grad, inverse)
    return (out, ga[:rank].T, gb[:rank], ga[rank:].T, gb[rank:])


def fits_one_head(mesh, args):
    hidden_states, w_query, a_query = args[0], args[1], args[4]
    n = mesh.shape["ctx"]
    heads_here = w_query.shape[1] // HEAD_DIM
    rows = hidden_states.shape[0]
    members = n * mesh.shape["head"] * mesh.shape["sub"]
    return (
        mesh.shape["rep"] == 2
        and mesh.shape["head"] == 2
        and mesh.shape["sub"] == 2
        and heads_here == n
        and HEAD_DIM == LANES
        and a_query.shape[1] == 8
        and rows % LANES == 0
        and rows // LANES <= 8
        and 2 * rows * n // LANES == members
        and rows * n * a_query.shape[0] <= 2**22
    )


def choose(mesh, *args):
    return one_head(*args) if fits_one_head(mesh, args) else local(*args)


def solution(mesh):
    in_specs = (
        P(("rep", "ctx"), ("head", "sub")),
        P("ctx", ("head", "sub")),
        P("ctx", ("head", "sub")),
        P("ctx", ("head", "sub")),
        P(),
        P(),
        P(None, ("head", "sub")),
        P(None, ("head", "sub")),
        P(("rep", "ctx")),
        P(("rep", "ctx"), ("head", "sub")),
    )
    out_specs = (
        P(("rep", "ctx"), ("head", "sub")),
        P(None, "rep"),
        P("rep", ("head", "sub")),
        P(None, "rep"),
        P("rep", ("head", "sub")),
    )
    return jax.shard_map(
        functools.partial(choose, mesh), mesh=mesh, in_specs=in_specs, out_specs=out_specs, check_vma=False
    )
```

```python
import functools
import math

import jax
import jax.numpy as jnp
from jax import lax
from jax.experimental import pallas as pl
from jax.experimental.pallas import tpu as pltpu
from jax.sharding import PartitionSpec as P

HEAD_DIM = 128
HEADS = 16
TRAIN_CTX = 4096
MAX_POS = 100000


def passed_along(block, axis, distance):
    devices = range(lax.axis_size(axis))
    route = [((i - distance) % len(devices), i) for i in devices]
    return lax.ppermute(block, axis, route)


def rope_tables(positions):
    half_dim = HEAD_DIM // 2
    inverse = jnp.exp(
        jnp.arange(half_dim, dtype=jnp.float32) * (-2.0 * math.log(10000.0) / HEAD_DIM)
    )
    scaled = positions.astype(jnp.float32) * (TRAIN_CTX / MAX_POS)
    angle = scaled[:, None] * inverse[None, :]
    return (jnp.cos(angle)[:, None, :], jnp.sin(angle)[:, None, :])


def rotate(vectors, cosine, sine):
    half_dim = vectors.shape[-1] // 2
    first = vectors[..., :half_dim]
    second = vectors[..., half_dim:]
    return jnp.concatenate(
        [first * cosine - second * sine, second * cosine + first * sine], axis=-1
    )


def project_back(features, low_grads):
    block_width = min(features.shape[1], 512)
    block_count = features.shape[1] // block_width

    def one_block(number):
        section = lax.dynamic_slice_in_dim(features, number * block_width, block_width, 1).astype(
            jnp.float32
        )
        return lax.dot_general(
            section, low_grads, (((0,), (0,)), ((), ())), precision=lax.Precision.HIGHEST
        )

    blocks = lax.map(one_block, jnp.arange(block_count))
    return blocks.reshape(features.shape[1], low_grads.shape[1])


def local(
    hidden_states, w_query, w_key, w_value, a_query, a_value, b_query, b_value, positions, out_grad
):
    rows_here = hidden_states.shape[0]
    columns = w_query.shape[1]
    heads_here = columns // HEAD_DIM
    rank_cols = a_query.shape[1]
    scale = 1.0 / math.sqrt(HEAD_DIM)
    shard_count = lax.axis_size("ctx")
    total_tokens = rows_here * shard_count
    group_len = total_tokens // 4
    reach = (group_len // 2 % rows_here + group_len - 1) // rows_here
    full_states = lax.all_gather(hidden_states, ("head", "sub"), axis=1, tiled=True)
    pieces = (
        lax.all_gather(w_query, "ctx", axis=0, tiled=True),
        lax.all_gather(w_key, "ctx", axis=0, tiled=True),
        lax.all_gather(w_value, "ctx", axis=0, tiled=True),
    )
    base_q, base_k, base_v = tuple(
        (
            jnp.dot(full_states, weights_piece, preferred_element_type=jnp.float32)
            for weights_piece in pieces
        )
    )
    low_q = jnp.dot(full_states, a_query, preferred_element_type=jnp.float32).astype(jnp.bfloat16)
    low_v = jnp.dot(full_states, a_value, preferred_element_type=jnp.float32).astype(jnp.bfloat16)
    cosine, sine = rope_tables(positions)
    pre_q = base_q + 2.0 * jnp.dot(low_q, b_query, preferred_element_type=jnp.float32)
    queries = rotate(pre_q.reshape(rows_here, heads_here, HEAD_DIM), cosine, sine).astype(
        jnp.bfloat16
    )
    keyed = rotate(base_k.reshape(rows_here, heads_here, HEAD_DIM), cosine, sine).astype(
        jnp.bfloat16
    )
    valued = (base_v + 2.0 * jnp.dot(low_v, b_value, preferred_element_type=jnp.float32)).astype(
        jnp.bfloat16
    )
    valued = valued.reshape(rows_here, heads_here, HEAD_DIM)
    current = jnp.stack([keyed, valued])
    collected = [current]
    for level in range(reach):
        current = passed_along(current, "ctx", 1)
        collected.append(current)
    key_rows = jnp.concatenate([block[0] for block in collected], axis=0)
    value_rows = jnp.concatenate([block[1] for block in collected], axis=0)
    shard_id = lax.axis_index("ctx")
    head_ids = lax.axis_index(("head", "sub")) * heads_here + jnp.arange(heads_here)
    amount = jnp.where(head_ids >= HEADS // 2, group_len // 2, 0).astype(jnp.int32)
    query_pos = shard_id * rows_here + jnp.arange(rows_here, dtype=jnp.int32)
    block_ids = jnp.arange(reach + 1, dtype=jnp.int32)
    source_shard = (shard_id - block_ids) % shard_count
    key_pos = (
        source_shard[:, None] * rows_here + jnp.arange(rows_here, dtype=jnp.int32)[None, :]
    ).reshape(-1)
    query_num = (query_pos[None, :] - amount[:, None]) % total_tokens
    key_num = (key_pos[None, :] - amount[:, None]) % total_tokens
    same_group = key_num[:, None, :] // group_len == query_num[:, :, None] // group_len
    visible = same_group & (key_num[:, None, :] <= query_num[:, :, None])
    scores = (
        jnp.einsum("qhd,khd->hqk", queries, key_rows, preferred_element_type=jnp.float32) * scale
    )
    scores = jnp.where(visible, scores, -jnp.inf)
    highest = jnp.max(scores, axis=-1, keepdims=True)
    expo = jnp.where(visible, jnp.exp(scores - highest), 0.0)
    probs = expo / jnp.sum(expo, axis=-1, keepdims=True)
    probs_b = probs.astype(jnp.bfloat16)
    attended = jnp.einsum("hqk,khd->qhd", probs_b, value_rows, preferred_element_type=jnp.float32)
    attn_out = attended.astype(jnp.bfloat16)
    grads = out_grad.reshape(rows_here, heads_here, HEAD_DIM)
    dprob = jnp.einsum("qhd,khd->hqk", grads, value_rows, preferred_element_type=jnp.float32)
    delta = jnp.sum(grads.astype(jnp.float32) * attn_out.astype(jnp.float32), axis=-1)
    dscore = probs * (dprob - delta.T[:, :, None])
    dscore_b = (dscore * scale).astype(jnp.bfloat16)
    dquery = jnp.einsum("hqk,khd->qhd", dscore_b, key_rows, preferred_element_type=jnp.float32)
    dvalue = jnp.einsum("hqk,qhd->khd", probs_b, grads, preferred_element_type=jnp.float32)
    value_blocks = dvalue.reshape(reach + 1, rows_here, columns)
    carried = value_blocks[reach]
    for level in range(reach, 0, -1):
        carried = passed_along(carried, "ctx", -1) + value_blocks[level - 1]
    dv_local = carried.astype(jnp.bfloat16)
    dq_local = rotate(dquery, cosine, -sine).astype(jnp.bfloat16).reshape(rows_here, columns)
    grad_bq = 2.0 * jnp.dot(low_q.T, dq_local, preferred_element_type=jnp.float32)
    grad_bv = 2.0 * jnp.dot(low_v.T, dv_local, preferred_element_type=jnp.float32)
    low_grads = jnp.concatenate(
        [
            2.0 * jnp.dot(dq_local, b_query.T, preferred_element_type=jnp.float32),
            2.0 * jnp.dot(dv_local, b_value.T, preferred_element_type=jnp.float32),
        ],
        axis=1,
    )
    grad_down = lax.psum(project_back(full_states, low_grads), ("ctx", "head", "sub"))
    grad_bq, grad_bv = lax.psum((grad_bq, grad_bv), "ctx")
    return (
        attn_out.reshape(rows_here, columns),
        grad_down[:, :rank_cols],
        grad_bq,
        grad_down[:, rank_cols:],
        grad_bv,
    )


LANES = 128
MESH = pl.DeviceIdType.MESH


def one_head_kernel(
    n,
    subs,
    wide,
    hid_ref,
    wq_ref,
    wk_ref,
    wv_ref,
    aq_ref,
    av_ref,
    bq_ref,
    bv_ref,
    pos_ref,
    og_ref,
    out_ref,
    gaq_ref,
    gbq_ref,
    gav_ref,
    gbv_ref,
    hbuf,
    wbuf,
    ogbuf,
    posbuf,
    ctab,
    stab,
    qbuf,
    kbuf,
    vbuf,
    acc,
    lowbuf,
    dqbuf,
    dvbuf,
    obuf,
    outbuf,
    gbsend,
    gbrecv,
    rsend,
    rrecv,
    total,
    agbuf,
    local_sem,
    hz_send,
    hx_send,
    hs_send,
    h_recv,
    w_send,
    wy_send,
    w_recv,
    og_send,
    og_recv,
    pos_send,
    pos_recv,
    out_send,
    out_recv,
    gb_send,
    gb_recv,
    rs_send,
    rs_recv,
    ag_send,
    ag_recv,
):
    f32, bf16 = jnp.float32, jnp.bfloat16
    rows, width = hid_ref.shape
    depth = wq_ref.shape[0]
    half = depth // 2
    tokens = rows * n
    group = tokens // 4
    r, c = lax.axis_index("rep"), lax.axis_index("ctx")
    h, s = lax.axis_index("head"), lax.axis_index("sub")
    hs = h * subs + s
    members = n * wide
    me = c * wide + hs
    weights = (wq_ref, wk_ref, wv_ref)
    pending = []
    dot_t = functools.partial(
        lax.dot_general, dimension_numbers=(((1,), (1,)), ((), ())), preferred_element_type=f32
    )
    t_dot = functools.partial(
        lax.dot_general, dimension_numbers=(((0,), (0,)), ((), ())), preferred_element_type=f32
    )

    def member(number):
        col = lax.rem(number, wide)
        return {"ctx": number // wide, "head": col // subs, "sub": lax.rem(col, subs)}

    def remote(src, dst, send, recv, device):
        return pltpu.make_async_remote_copy(
            src_ref=src, dst_ref=dst, send_sem=send, recv_sem=recv, device_id=device, device_id_type=MESH
        )

    def launch(copy, cond=None):
        if cond is None:
            copy.start()
        else:
            pl.when(cond)(copy.start)
        pending.append((copy, cond))

    barrier = pltpu.get_barrier_semaphore()
    for k in range(1, members):
        pl.semaphore_signal(
            barrier, inc=1, device_id=member(lax.rem(me + k, members)), device_id_type=MESH
        )
    pl.semaphore_signal(barrier, inc=1, device_id={"rep": 1 - r}, device_id_type=MESH)

    def cols(number, size):
        return pl.ds(pl.multiple_of(number * size, LANES), size)

    def part(number, size):
        return pl.ds(pl.multiple_of(number * size, 8), size)

    def hblk(block, column):
        return hbuf.at[part(block, rows), cols(column, width)]

    def wblk(block, which, side):
        return wbuf.at[
            pl.ds(pl.multiple_of(block * depth + side * half, 8), half), pl.ds(which * LANES, LANES)
        ]

    locals_ = [
        pltpu.make_async_copy(hid_ref, hblk(c, hs), local_sem.at[0]),
        pltpu.make_async_copy(og_ref.at[:, cols(c, LANES)], ogbuf.at[part(c, rows), :], local_sem.at[1]),
        pltpu.make_async_copy(pos_ref, posbuf.at[c], local_sem.at[2]),
    ]
    for m in range(3):
        locals_.append(
            pltpu.make_async_copy(
                weights[m].at[:, cols(c, LANES)],
                wbuf.at[part(c, depth), pl.ds(m * LANES, LANES)],
                local_sem.at[3 + m],
            )
        )
    for copy in locals_:
        copy.start()
    pl.semaphore_wait(barrier, members)

    def spread(src, block):
        launch(
            remote(src, hblk(block, hs), hx_send.at[block], h_recv.at[block, hs], {"head": 1 - h})
        )
        launch(
            remote(src, hblk(block, hs), hs_send.at[0, block], h_recv.at[block, hs], {"sub": 1 - s})
        )

    def arrived(block, column):
        return remote(
            hblk(block, column), hblk(block, column), hx_send.at[0], h_recv.at[block, column], {"sub": 1 - s}
        )

    def go_up(src, block):
        return remote(src, hblk(block, hs), hz_send.at[0, block], h_recv.at[block, hs], {"ctx": c + 1})

    def go_down(src, block):
        return remote(src, hblk(block, hs), hz_send.at[1, block], h_recv.at[block, hs], {"ctx": c - 1})

    def send_w(t, sign):
        target = c + sign * t
        cond = (target < n) if sign > 0 else (target >= 0)
        slot = 2 * (t - 1) + (1 if sign > 0 else 0)
        for m in range(3):
            launch(
                remote(
                    weights[m].at[pl.ds(pl.multiple_of(r * half, 8), half), cols(target, LANES)],
                    wblk(c, m, r),
                    w_send.at[slot, m],
                    w_recv.at[c, m, r],
                    {"ctx": target},
                ),
                cond,
            )

    def pass_w(block, cond):
        for m in range(3):
            copy = remote(
                wblk(block, m, r), wblk(block, m, r), wy_send.at[block, m], w_recv.at[block, m, r], {"rep": 1 - r}
            )

            @pl.when(cond)
            def _():
                copy.wait_recv()
                copy.start()

            pending.append((copy, cond))

    def pass_x(block, cond):
        copy = remote(
            hblk(block, (1 - h) * subs + s),
            hblk(block, (1 - h) * subs + s),
            hs_send.at[1, block],
            h_recv.at[block, (1 - h) * subs + s],
            {"sub": 1 - s},
        )

        def act():
            copy.wait_recv()
            copy.start()

        if cond is None:
            act()
        else:
            pl.when(cond)(act)
        pending.append((copy, cond))

    launch(go_up(hid_ref, c), c < n - 1)
    launch(go_down(hid_ref, c), c > 0)
    spread(hid_ref, c)
    def routes():
        for t in range(1, n):
            for sign in (1, -1):
                target = c + sign * t
                cond = (target < n) if sign > 0 else (target >= 0)
                yield 2 * (t - 1) + (1 if sign > 0 else 0), target, cond

    for slot, target, cond in routes():
        launch(remote(pos_ref, posbuf.at[c], pos_send.at[slot], pos_recv.at[c], {"ctx": target}), cond)

    def hidden_step(t):
        low_block, high_block = c - t, c + t

        @pl.when(low_block >= 0)
        def _():
            arrived(low_block, hs).wait_recv()

        for copy_of, block, cond, more in (
            (go_up, low_block, low_block >= 0, c < n - 1),
            (go_down, high_block, high_block < n, c > 0),
        ):
            if copy_of is go_down:

                @pl.when(cond)
                def _():
                    arrived(high_block, hs).wait_recv()

            launch(copy_of(hblk(block, hs), block), cond & more)
            for copy in (
                remote(hblk(block, hs), hblk(block, hs), hx_send.at[block], h_recv.at[block, hs], {"head": 1 - h}),
                remote(hblk(block, hs), hblk(block, hs), hs_send.at[0, block], h_recv.at[block, hs], {"sub": 1 - s}),
            ):
                launch(copy, cond)

    def x_step(t):
        pass_x(c - t, c - t >= 0)
        pass_x(c + t, c + t < n)

    def w_step(t):
        pass_w(c - t, c - t >= 0)
        pass_w(c + t, c + t < n)

    def tables():
        for block in range(n):

            @pl.when(block != c)
            def _():
                remote(pos_ref, posbuf.at[block], pos_send.at[0], pos_recv.at[block], {"sub": 1 - s}).wait_recv()

        locals_[2].wait()
        lane = lax.broadcasted_iota(jnp.int32, (LANES, LANES), 1)
        chunks = rows // LANES
        half_dim = LANES // 2
        index = lax.broadcasted_iota(jnp.int32, (8, LANES), 1) % half_dim
        inverse = jnp.exp(index.astype(f32) * (-2.0 * math.log(10000.0) / HEAD_DIM))[0:1, :]

        def one(number, carry):
            row = posbuf[number // chunks, pl.ds(lax.rem(number, chunks), 1), :].astype(f32)
            column = jnp.transpose(jnp.broadcast_to(row, (LANES, LANES)))
            angle = (column * (TRAIN_CTX / MAX_POS)) * inverse
            here = part(number, LANES)
            ctab[here, :] = jnp.cos(angle)
            sine = jnp.sin(angle)
            stab[here, :] = jnp.where(lane < LANES // 2, -sine, sine)
            return carry

        lax.fori_loop(0, tokens // LANES, one, 0)

    hidden_step(1)
    send_w(1, 1)
    send_w(1, -1)
    pass_x(c, None)
    for t in range(2, n):
        hidden_step(t)
        if t == 2:
            for far in range(2, n):
                send_w(far, 1)
                send_w(far, -1)
            for slot, target, cond in routes():
                launch(
                    remote(
                        og_ref.at[:, cols(target, LANES)],
                        ogbuf.at[part(c, rows), :],
                        og_send.at[slot],
                        og_recv.at[c],
                        {"ctx": target},
                    ),
                    cond,
                )
        x_step(t - 1)
        w_step(t - 1)
        if t == 2:
            tables()
    x_step(n - 1)
    for block in range(n):
        for column in range(wide):
            mine = (column // subs == h) & (column % subs == s)
            across = (column // subs != h) & (column % subs == s)

            @pl.when(jnp.logical_not(mine | across))
            def _():
                arrived(block, column).wait_recv()

    for number, copy in enumerate(locals_):
        if number != 2:
            copy.wait()

    def gather_low(block, carry):
        here = part(block, rows)
        a_both = jnp.concatenate([aq_ref[...].astype(f32), av_ref[...].astype(f32)], axis=0).astype(bf16)
        lowbuf[here, :] = dot_t(hbuf[here, :], a_both).astype(bf16)
        return carry

    def multiply(slice_, fresh):
        deep = cols(slice_, depth)

        def rows_of(block, carry):
            here = part(block, rows)
            y = jnp.dot(hbuf[here, deep], wbuf[part(slice_, depth), :], preferred_element_type=f32)
            if fresh:
                acc[here, :] = y
            else:
                acc[here, :] += y
            return carry

        lax.fori_loop(0, n, rows_of, 0)

    lax.fori_loop(0, n, gather_low, 0)
    multiply(c, True)
    w_step(n - 1)
    for t in range(1, n):
        for block, cond in ((c - t, c - t >= 0), (c + t, c + t < n)):

            @pl.when(cond)
            def _():
                for m in range(3):
                    remote(
                        wblk(block, m, 1 - r),
                        wblk(block, m, 1 - r),
                        wy_send.at[0, 0],
                        w_recv.at[block, m, 1 - r],
                        {"rep": 1 - r},
                    ).wait_recv()
                multiply(block, False)

    for block in range(n):

        @pl.when(block != c)
        def _():
            remote(
                ogbuf.at[part(block, rows), :], ogbuf.at[part(block, rows), :], og_send.at[0], og_recv.at[block], {"sub": 1 - s}
            ).wait_recv()

    def turn(u, cosine, sine):
        return u * cosine + pltpu.roll(u, LANES // 2, 1) * sine

    empty = jnp.zeros((8, LANES), f32)
    bq = jnp.concatenate([bq_ref[:, cols(c, LANES)].astype(f32), empty], axis=0).astype(bf16)
    bv = jnp.concatenate([empty, bv_ref[:, cols(c, LANES)].astype(f32)], axis=0).astype(bf16)

    def project(block, carry):
        here = part(block, rows)
        y = acc[here, :]
        low = lowbuf[here, :]
        cosine, sine = ctab[here, :], stab[here, :]
        pre_q = y[:, :LANES] + 2.0 * jnp.dot(low, bq, preferred_element_type=f32)
        qbuf[here, :] = turn(pre_q, cosine, sine).astype(bf16)
        kbuf[here, :] = turn(y[:, LANES : 2 * LANES], cosine, sine).astype(bf16)
        vbuf[here, :] = (
            y[:, 2 * LANES : 3 * LANES] + 2.0 * jnp.dot(low, bv, preferred_element_type=f32)
        ).astype(bf16)
        return carry

    lax.fori_loop(0, n, project, 0)

    shift = jnp.where(hs * n + c >= HEADS // 2, group // 2, 0)
    scale = 1.0 / math.sqrt(HEAD_DIM)
    hg = group // 2
    allowed = lax.broadcasted_iota(jnp.int32, (group, group), 0) >= lax.broadcasted_iota(
        jnp.int32, (group, group), 1
    )

    def attend(g, carry):
        first = pl.ds(pl.multiple_of(lax.rem(g * group + shift, tokens), 8), hg)
        second = pl.ds(pl.multiple_of(lax.rem(g * group + hg + shift, tokens), 8), hg)

        def take(ref):
            return jnp.concatenate([ref[first, :], ref[second, :]], axis=0)

        def put(ref, value):
            ref[first, :] = value[:hg]
            ref[second, :] = value[hg:]

        q, k, v, grad = take(qbuf), take(kbuf), take(vbuf), take(ogbuf)
        scores = jnp.where(allowed, dot_t(q, k) * scale, -jnp.inf)
        highest = jnp.max(scores, axis=-1, keepdims=True)
        expo = jnp.where(allowed, jnp.exp(scores - highest), 0.0)
        probs = expo / jnp.sum(expo, axis=-1, keepdims=True)
        probs_b = probs.astype(bf16)
        out = jnp.dot(probs_b, v, preferred_element_type=f32).astype(bf16)
        put(obuf, out)
        dprob = dot_t(grad, v)
        delta = jnp.sum(grad.astype(f32) * out.astype(f32), axis=-1, keepdims=True)
        dscore_b = (probs * (dprob - delta) * scale).astype(bf16)
        dq = jnp.dot(dscore_b, k, preferred_element_type=f32)
        put(dqbuf, turn(dq, take(ctab), -take(stab)).astype(bf16))
        put(dvbuf, t_dot(probs_b, grad).astype(bf16))
        return carry

    lax.fori_loop(0, tokens // group, attend, 0)

    dq, dv, low = dqbuf[...], dvbuf[...], lowbuf[...]
    low_t = 2.0 * (dot_t(bq, dq) + dot_t(bv, dv))
    for k in range(members):
        at = (k // 2) * LANES
        rsend[k] = low_t[8 * (k % 2) : 8 * (k % 2) + 8, at : at + LANES]
    for k in range(1, members):
        to = lax.rem(me + k, members)
        launch(remote(rsend.at[to], rrecv.at[me], rs_send.at[k], rs_recv.at[me], member(to)))
    gbsend[0:8, :] = (2.0 * t_dot(low, dq))[0:8]
    gbsend[8:16, :] = (2.0 * t_dot(low, dv))[8:16]
    for slot, target, cond in routes():
        launch(
            remote(
                obuf.at[part(target, rows), :], outbuf.at[c], out_send.at[slot], out_recv.at[c], {"ctx": target}
            ),
            cond,
        )
    for slot, target, cond in routes():
        launch(remote(gbsend, gbrecv.at[c], gb_send.at[slot], gb_recv.at[c], {"ctx": target}), cond)
    out_ref[:, cols(c, LANES)] = obuf[part(c, rows), :]
    gbq_ref[:, cols(c, LANES)] = gbsend[0:8, :]
    gbv_ref[:, cols(c, LANES)] = gbsend[8:16, :]

    rrecv[me] = rsend[me]
    for k in range(1, members):
        frm = lax.rem(me + k, members)
        remote(rsend.at[0], rrecv.at[frm], rs_send.at[0], rs_recv.at[frm], {"sub": 1 - s}).wait_recv()
    reduced = rrecv[0]
    for k in range(1, members):
        reduced = reduced + rrecv[k]
    total[...] = reduced
    agbuf[me] = reduced
    for k in range(1, members):
        to = lax.rem(me + k, members)
        launch(remote(total, agbuf.at[me], ag_send.at[k], ag_recv.at[me], member(to)))
    for k in range(1, members):
        frm = lax.rem(me + k, members)
        remote(total, agbuf.at[frm], ag_send.at[0], ag_recv.at[frm], {"sub": 1 - s}).wait_recv()
    full = jnp.concatenate(
        [
            jnp.concatenate([agbuf[2 * k + side] for k in range(members // 2)], axis=1)
            for side in range(2)
        ],
        axis=0,
    )
    upper = full.astype(bf16)
    lower = (full - upper.astype(f32)).astype(bf16)
    both = jnp.concatenate([upper, lower], axis=0)
    tile = 512

    def back(number, carry):
        here = pl.ds(pl.multiple_of(number * tile, LANES), tile)
        product = jnp.dot(both, hbuf[:, here], preferred_element_type=f32)
        gaq_ref[:, here] = product[0:8] + product[16:24]
        gav_ref[:, here] = product[8:16] + product[24:32]
        return carry

    lax.fori_loop(0, hbuf.shape[1] // tile, back, 0)
    for block in range(n):

        @pl.when(block != c)
        def _():
            remote(gbsend, gbrecv.at[block], gb_send.at[0], gb_recv.at[block], {"sub": 1 - s}).wait_recv()
            remote(outbuf.at[block], outbuf.at[block], out_send.at[0], out_recv.at[block], {"sub": 1 - s}).wait_recv()
            gbq_ref[:, block * LANES : (block + 1) * LANES] = gbrecv[block, 0:8, :]
            gbv_ref[:, block * LANES : (block + 1) * LANES] = gbrecv[block, 8:16, :]
            out_ref[:, block * LANES : (block + 1) * LANES] = outbuf[block]

    for copy, cond in pending:
        if cond is None:
            copy.wait_send()
        else:
            pl.when(cond)(copy.wait_send)


def one_head(
    hidden_states, w_query, w_key, w_value, a_query, a_value, b_query, b_value, positions, out_grad
):
    f32, bf16 = jnp.float32, jnp.bfloat16
    n, subs = lax.axis_size("ctx"), lax.axis_size("sub")
    wide = subs * lax.axis_size("head")
    rows, width = hidden_states.shape
    model = a_query.shape[0]
    rank = a_query.shape[1]
    tokens = rows * n
    columns = w_query.shape[1]
    members = n * wide
    pos = positions.reshape(rows // LANES, LANES)
    vmem, dma = pltpu.VMEM, pltpu.SemaphoreType.DMA
    hbm_spec = pl.BlockSpec(memory_space=pl.ANY)
    vmem_spec = pl.BlockSpec(memory_space=pltpu.VMEM)
    out, gaq, gbq, gav, gbv = pl.pallas_call(
        functools.partial(one_head_kernel, n, subs, wide),
        out_shape=(
            jax.ShapeDtypeStruct((rows, columns), bf16),
            jax.ShapeDtypeStruct((rank, model), f32),
            jax.ShapeDtypeStruct((rank, columns), f32),
            jax.ShapeDtypeStruct((rank, model), f32),
            jax.ShapeDtypeStruct((rank, columns), f32),
        ),
        in_specs=[hbm_spec] * 4 + [vmem_spec] * 4 + [hbm_spec] * 2,
        out_specs=[vmem_spec] * 5,
        scratch_shapes=[
            vmem((tokens, model), bf16),
            vmem((model, 3 * LANES), bf16),
            vmem((tokens, LANES), bf16),
            vmem((n, rows // LANES, LANES), jnp.int32),
            vmem((tokens, LANES), f32),
            vmem((tokens, LANES), f32),
            vmem((tokens, LANES), bf16),
            vmem((tokens, LANES), bf16),
            vmem((tokens, LANES), bf16),
            vmem((tokens, 3 * LANES), f32),
            vmem((tokens, 2 * rank), bf16),
            vmem((tokens, LANES), bf16),
            vmem((tokens, LANES), bf16),
            vmem((tokens, LANES), bf16),
            vmem((n, rows, LANES), bf16),
            vmem((2 * rank, LANES), f32),
            vmem((n, 2 * rank, LANES), f32),
            vmem((members, 8, LANES), f32),
            vmem((members, 8, LANES), f32),
            vmem((8, LANES), f32),
            vmem((members, 8, LANES), f32),
            dma((6,)),
            dma((2, n)),
            dma((n,)),
            dma((2, n)),
            dma((n, wide)),
            dma((2 * n, 3)),
            dma((n, 3)),
            dma((n, 3, 2)),
            dma((2 * n,)),
            dma((n,)),
            dma((2 * n,)),
            dma((n,)),
            dma((2 * n,)),
            dma((n,)),
            dma((2 * n,)),
            dma((n,)),
            dma((members,)),
            dma((members,)),
            dma((members,)),
            dma((members,)),
        ],
        compiler_params=pltpu.CompilerParams(
            collective_id=0, has_side_effects=True, vmem_limit_bytes=56 * 1024 * 1024
        ),
    )(
        hidden_states, w_query, w_key, w_value, a_query.T, a_value.T, b_query, b_value, pos, out_grad
    )
    return (out, gaq.T, gbq, gav.T, gbv)


def fits_one_head(mesh, args):
    hidden_states, w_query, a_query = args[0], args[1], args[4]
    n = mesh.shape["ctx"]
    heads_here = w_query.shape[1] // HEAD_DIM
    rows = hidden_states.shape[0]
    members = n * mesh.shape["head"] * mesh.shape["sub"]
    return (
        mesh.shape["rep"] == 2
        and mesh.shape["head"] == 2
        and mesh.shape["sub"] == 2
        and heads_here == n
        and HEAD_DIM == LANES
        and a_query.shape[1] == 8
        and rows % LANES == 0
        and rows // LANES <= 8
        and 2 * rows * n // LANES == members
        and rows * n * a_query.shape[0] <= 2**22
    )


def choose(mesh, *args):
    return one_head(*args) if fits_one_head(mesh, args) else local(*args)


def solution(mesh):
    in_specs = (
        P(("rep", "ctx"), ("head", "sub")),
        P("ctx", ("head", "sub")),
        P("ctx", ("head", "sub")),
        P("ctx", ("head", "sub")),
        P(),
        P(),
        P(None, ("head", "sub")),
        P(None, ("head", "sub")),
        P(("rep", "ctx")),
        P(("rep", "ctx"), ("head", "sub")),
    )
    out_specs = (
        P(("rep", "ctx"), ("head", "sub")),
        P(None, "rep"),
        P("rep", ("head", "sub")),
        P(None, "rep"),
        P("rep", ("head", "sub")),
    )
    return jax.shard_map(
        functools.partial(choose, mesh), mesh=mesh, in_specs=in_specs, out_specs=out_specs, check_vma=False
    )
```

```python
import functools
import math

import jax
import jax.numpy as jnp
from jax import lax
from jax.experimental import pallas as pl
from jax.experimental.pallas import tpu as pltpu
from jax.sharding import PartitionSpec as P

HEAD_DIM = 128
HEADS = 16
TRAIN_CTX = 4096
MAX_POS = 100000


def passed_along(block, axis, distance):
    devices = range(lax.axis_size(axis))
    route = [((i - distance) % len(devices), i) for i in devices]
    return lax.ppermute(block, axis, route)


def rope_tables(positions):
    half_dim = HEAD_DIM // 2
    inverse = jnp.exp(
        jnp.arange(half_dim, dtype=jnp.float32) * (-2.0 * math.log(10000.0) / HEAD_DIM)
    )
    scaled = positions.astype(jnp.float32) * (TRAIN_CTX / MAX_POS)
    angle = scaled[:, None] * inverse[None, :]
    return (jnp.cos(angle)[:, None, :], jnp.sin(angle)[:, None, :])


def rotate(vectors, cosine, sine):
    half_dim = vectors.shape[-1] // 2
    first = vectors[..., :half_dim]
    second = vectors[..., half_dim:]
    return jnp.concatenate(
        [first * cosine - second * sine, second * cosine + first * sine], axis=-1
    )


def project_back(features, low_grads):
    block_width = min(features.shape[1], 512)
    block_count = features.shape[1] // block_width

    def one_block(number):
        section = lax.dynamic_slice_in_dim(features, number * block_width, block_width, 1).astype(
            jnp.float32
        )
        return lax.dot_general(
            section, low_grads, (((0,), (0,)), ((), ())), precision=lax.Precision.HIGHEST
        )

    blocks = lax.map(one_block, jnp.arange(block_count))
    return blocks.reshape(features.shape[1], low_grads.shape[1])


def local(
    hidden_states, w_query, w_key, w_value, a_query, a_value, b_query, b_value, positions, out_grad
):
    rows_here = hidden_states.shape[0]
    columns = w_query.shape[1]
    heads_here = columns // HEAD_DIM
    rank_cols = a_query.shape[1]
    scale = 1.0 / math.sqrt(HEAD_DIM)
    shard_count = lax.axis_size("ctx")
    total_tokens = rows_here * shard_count
    group_len = total_tokens // 4
    reach = (group_len // 2 % rows_here + group_len - 1) // rows_here
    full_states = lax.all_gather(hidden_states, ("head", "sub"), axis=1, tiled=True)
    pieces = (
        lax.all_gather(w_query, "ctx", axis=0, tiled=True),
        lax.all_gather(w_key, "ctx", axis=0, tiled=True),
        lax.all_gather(w_value, "ctx", axis=0, tiled=True),
    )
    base_q, base_k, base_v = tuple(
        (
            jnp.dot(full_states, weights_piece, preferred_element_type=jnp.float32)
            for weights_piece in pieces
        )
    )
    low_q = jnp.dot(full_states, a_query, preferred_element_type=jnp.float32).astype(jnp.bfloat16)
    low_v = jnp.dot(full_states, a_value, preferred_element_type=jnp.float32).astype(jnp.bfloat16)
    cosine, sine = rope_tables(positions)
    pre_q = base_q + 2.0 * jnp.dot(low_q, b_query, preferred_element_type=jnp.float32)
    queries = rotate(pre_q.reshape(rows_here, heads_here, HEAD_DIM), cosine, sine).astype(
        jnp.bfloat16
    )
    keyed = rotate(base_k.reshape(rows_here, heads_here, HEAD_DIM), cosine, sine).astype(
        jnp.bfloat16
    )
    valued = (base_v + 2.0 * jnp.dot(low_v, b_value, preferred_element_type=jnp.float32)).astype(
        jnp.bfloat16
    )
    valued = valued.reshape(rows_here, heads_here, HEAD_DIM)
    current = jnp.stack([keyed, valued])
    collected = [current]
    for level in range(reach):
        current = passed_along(current, "ctx", 1)
        collected.append(current)
    key_rows = jnp.concatenate([block[0] for block in collected], axis=0)
    value_rows = jnp.concatenate([block[1] for block in collected], axis=0)
    shard_id = lax.axis_index("ctx")
    head_ids = lax.axis_index(("head", "sub")) * heads_here + jnp.arange(heads_here)
    amount = jnp.where(head_ids >= HEADS // 2, group_len // 2, 0).astype(jnp.int32)
    query_pos = shard_id * rows_here + jnp.arange(rows_here, dtype=jnp.int32)
    block_ids = jnp.arange(reach + 1, dtype=jnp.int32)
    source_shard = (shard_id - block_ids) % shard_count
    key_pos = (
        source_shard[:, None] * rows_here + jnp.arange(rows_here, dtype=jnp.int32)[None, :]
    ).reshape(-1)
    query_num = (query_pos[None, :] - amount[:, None]) % total_tokens
    key_num = (key_pos[None, :] - amount[:, None]) % total_tokens
    same_group = key_num[:, None, :] // group_len == query_num[:, :, None] // group_len
    visible = same_group & (key_num[:, None, :] <= query_num[:, :, None])
    scores = (
        jnp.einsum("qhd,khd->hqk", queries, key_rows, preferred_element_type=jnp.float32) * scale
    )
    scores = jnp.where(visible, scores, -jnp.inf)
    highest = jnp.max(scores, axis=-1, keepdims=True)
    expo = jnp.where(visible, jnp.exp(scores - highest), 0.0)
    probs = expo / jnp.sum(expo, axis=-1, keepdims=True)
    probs_b = probs.astype(jnp.bfloat16)
    attended = jnp.einsum("hqk,khd->qhd", probs_b, value_rows, preferred_element_type=jnp.float32)
    attn_out = attended.astype(jnp.bfloat16)
    grads = out_grad.reshape(rows_here, heads_here, HEAD_DIM)
    dprob = jnp.einsum("qhd,khd->hqk", grads, value_rows, preferred_element_type=jnp.float32)
    delta = jnp.sum(grads.astype(jnp.float32) * attn_out.astype(jnp.float32), axis=-1)
    dscore = probs * (dprob - delta.T[:, :, None])
    dscore_b = (dscore * scale).astype(jnp.bfloat16)
    dquery = jnp.einsum("hqk,khd->qhd", dscore_b, key_rows, preferred_element_type=jnp.float32)
    dvalue = jnp.einsum("hqk,qhd->khd", probs_b, grads, preferred_element_type=jnp.float32)
    value_blocks = dvalue.reshape(reach + 1, rows_here, columns)
    carried = value_blocks[reach]
    for level in range(reach, 0, -1):
        carried = passed_along(carried, "ctx", -1) + value_blocks[level - 1]
    dv_local = carried.astype(jnp.bfloat16)
    dq_local = rotate(dquery, cosine, -sine).astype(jnp.bfloat16).reshape(rows_here, columns)
    grad_bq = 2.0 * jnp.dot(low_q.T, dq_local, preferred_element_type=jnp.float32)
    grad_bv = 2.0 * jnp.dot(low_v.T, dv_local, preferred_element_type=jnp.float32)
    low_grads = jnp.concatenate(
        [
            2.0 * jnp.dot(dq_local, b_query.T, preferred_element_type=jnp.float32),
            2.0 * jnp.dot(dv_local, b_value.T, preferred_element_type=jnp.float32),
        ],
        axis=1,
    )
    grad_down = lax.psum(project_back(full_states, low_grads), ("ctx", "head", "sub"))
    grad_bq, grad_bv = lax.psum((grad_bq, grad_bv), "ctx")
    return (
        attn_out.reshape(rows_here, columns),
        grad_down[:, :rank_cols],
        grad_bq,
        grad_down[:, rank_cols:],
        grad_bv,
    )


LANES = 128
PIECES = 2
MESH = pl.DeviceIdType.MESH


def one_head_kernel(
    n,
    subs,
    wide,
    hid_ref,
    wq_ref,
    wk_ref,
    wv_ref,
    aq_ref,
    av_ref,
    bq_ref,
    bv_ref,
    pos_ref,
    og_ref,
    out_ref,
    gaq_ref,
    gbq_ref,
    gav_ref,
    gbv_ref,
    hbuf,
    wbuf,
    ogbuf,
    posbuf,
    ctab,
    stab,
    qbuf,
    kbuf,
    vbuf,
    acc,
    lowbuf,
    dqbuf,
    dvbuf,
    obuf,
    outbuf,
    gbsend,
    gbrecv,
    rsend,
    rrecv,
    total,
    agbuf,
    local_sem,
    hz_send,
    hx_send,
    hs_send,
    h_recv,
    w_send,
    wy_send,
    w_recv,
    og_send,
    og_recv,
    pos_send,
    pos_recv,
    out_send,
    out_recv,
    gb_send,
    gb_recv,
    rs_send,
    rs_recv,
    ag_send,
    ag_recv,
):
    f32, bf16 = jnp.float32, jnp.bfloat16
    rows, width = hid_ref.shape
    depth = wq_ref.shape[0]
    half = depth // 2
    tokens = rows * n
    group = tokens // 4
    r, c = lax.axis_index("rep"), lax.axis_index("ctx")
    h, s = lax.axis_index("head"), lax.axis_index("sub")
    hs = h * subs + s
    members = n * wide
    me = c * wide + hs
    weights = (wq_ref, wk_ref, wv_ref)
    pending = []
    dot_t = functools.partial(
        lax.dot_general, dimension_numbers=(((1,), (1,)), ((), ())), preferred_element_type=f32
    )
    t_dot = functools.partial(
        lax.dot_general, dimension_numbers=(((0,), (0,)), ((), ())), preferred_element_type=f32
    )

    def member(number):
        col = lax.rem(number, wide)
        return {"ctx": number // wide, "head": col // subs, "sub": lax.rem(col, subs)}

    def remote(src, dst, send, recv, device):
        return pltpu.make_async_remote_copy(
            src_ref=src, dst_ref=dst, send_sem=send, recv_sem=recv, device_id=device, device_id_type=MESH
        )

    def launch(copy, cond=None):
        if cond is None:
            copy.start()
        else:
            pl.when(cond)(copy.start)
        pending.append((copy, cond))

    barrier = pltpu.get_barrier_semaphore()
    for k in range(1, members):
        pl.semaphore_signal(
            barrier, inc=1, device_id=member(lax.rem(me + k, members)), device_id_type=MESH
        )
    pl.semaphore_signal(barrier, inc=1, device_id={"rep": 1 - r}, device_id_type=MESH)

    def cols(number, size):
        return pl.ds(pl.multiple_of(number * size, LANES), size)

    def part(number, size):
        return pl.ds(pl.multiple_of(number * size, 8), size)

    def hblk(block, column, piece):
        return hbuf.at[part(block * PIECES + piece, rows // PIECES), cols(column, width)]

    def own_piece(piece):
        return hid_ref.at[pl.ds(piece * (rows // PIECES), rows // PIECES), :]

    def wblk(block, which, side):
        return wbuf.at[
            pl.ds(pl.multiple_of(block * depth + side * half, 8), half), pl.ds(which * LANES, LANES)
        ]

    locals_ = [
        pltpu.make_async_copy(hid_ref, hbuf.at[part(c, rows), cols(hs, width)], local_sem.at[0]),
        pltpu.make_async_copy(og_ref.at[:, cols(c, LANES)], ogbuf.at[part(c, rows), :], local_sem.at[1]),
        pltpu.make_async_copy(pos_ref, posbuf.at[c], local_sem.at[2]),
    ]
    for m in range(3):
        locals_.append(
            pltpu.make_async_copy(
                weights[m].at[:, cols(c, LANES)],
                wbuf.at[part(c, depth), pl.ds(m * LANES, LANES)],
                local_sem.at[3 + m],
            )
        )
    for copy in locals_:
        copy.start()
    pl.semaphore_wait(barrier, members)

    def spread(src, block, piece, cond=None):
        land, got = hblk(block, hs, piece), h_recv.at[block, hs, piece]
        launch(remote(src, land, hx_send.at[block, piece], got, {"head": 1 - h}), cond)
        launch(remote(src, land, hs_send.at[0, block, piece], got, {"sub": 1 - s}), cond)

    def arrived(block, column, piece):
        land = hblk(block, column, piece)
        return remote(land, land, hx_send.at[0, 0], h_recv.at[block, column, piece], {"sub": 1 - s})

    def go_up(src, block, piece):
        return remote(
            src, hblk(block, hs, piece), hz_send.at[0, block, piece], h_recv.at[block, hs, piece], {"ctx": c + 1}
        )

    def go_down(src, block, piece):
        return remote(
            src, hblk(block, hs, piece), hz_send.at[1, block, piece], h_recv.at[block, hs, piece], {"ctx": c - 1}
        )

    def send_w(t, sign):
        target = c + sign * t
        cond = (target < n) if sign > 0 else (target >= 0)
        slot = 2 * (t - 1) + (1 if sign > 0 else 0)
        for m in range(3):
            launch(
                remote(
                    weights[m].at[pl.ds(pl.multiple_of(r * half, 8), half), cols(target, LANES)],
                    wblk(c, m, r),
                    w_send.at[slot, m],
                    w_recv.at[c, m, r],
                    {"ctx": target},
                ),
                cond,
            )

    def pass_w(block, cond):
        for m in range(3):
            copy = remote(
                wblk(block, m, r), wblk(block, m, r), wy_send.at[block, m], w_recv.at[block, m, r], {"rep": 1 - r}
            )

            @pl.when(cond)
            def _():
                copy.wait_recv()
                copy.start()

            pending.append((copy, cond))

    def pass_x(block, cond, piece):
        column = (1 - h) * subs + s
        land = hblk(block, column, piece)
        copy = remote(
            land, land, hs_send.at[1, block, piece], h_recv.at[block, column, piece], {"sub": 1 - s}
        )

        def act():
            copy.wait_recv()
            copy.start()

        if cond is None:
            act()
        else:
            pl.when(cond)(act)
        pending.append((copy, cond))

    for piece in range(PIECES):
        launch(go_up(own_piece(piece), c, piece), c < n - 1)
        launch(go_down(own_piece(piece), c, piece), c > 0)
        spread(own_piece(piece), c, piece)

    def routes():
        for t in range(1, n):
            for sign in (1, -1):
                target = c + sign * t
                cond = (target < n) if sign > 0 else (target >= 0)
                yield 2 * (t - 1) + (1 if sign > 0 else 0), target, cond

    for slot, target, cond in routes():
        launch(remote(pos_ref, posbuf.at[c], pos_send.at[slot], pos_recv.at[c], {"ctx": target}), cond)

    def hidden_step(t):
        for piece in range(PIECES):
            for go, block, cond, more in (
                (go_up, c - t, c - t >= 0, c < n - 1),
                (go_down, c + t, c + t < n, c > 0),
            ):
                pl.when(cond)(arrived(block, hs, piece).wait_recv)
                launch(go(hblk(block, hs, piece), block, piece), cond & more)
                spread(hblk(block, hs, piece), block, piece, cond)

    def x_step(t):
        for piece in range(PIECES):
            pass_x(c - t, c - t >= 0, piece)
            pass_x(c + t, c + t < n, piece)

    def w_step(t):
        pass_w(c - t, c - t >= 0)
        pass_w(c + t, c + t < n)

    def tables():
        for block in range(n):

            @pl.when(block != c)
            def _():
                remote(pos_ref, posbuf.at[block], pos_send.at[0], pos_recv.at[block], {"sub": 1 - s}).wait_recv()

        locals_[2].wait()
        lane = lax.broadcasted_iota(jnp.int32, (LANES, LANES), 1)
        chunks = rows // LANES
        half_dim = LANES // 2
        index = lax.broadcasted_iota(jnp.int32, (8, LANES), 1) % half_dim
        inverse = jnp.exp(index.astype(f32) * (-2.0 * math.log(10000.0) / HEAD_DIM))[0:1, :]

        def one(number, carry):
            row = posbuf[number // chunks, pl.ds(lax.rem(number, chunks), 1), :].astype(f32)
            column = jnp.transpose(jnp.broadcast_to(row, (LANES, LANES)))
            angle = (column * (TRAIN_CTX / MAX_POS)) * inverse
            here = part(number, LANES)
            ctab[here, :] = jnp.cos(angle)
            sine = jnp.sin(angle)
            stab[here, :] = jnp.where(lane < LANES // 2, -sine, sine)
            return carry

        lax.fori_loop(0, tokens // LANES, one, 0)

    send_w(1, 1)
    send_w(1, -1)
    hidden_step(1)
    for piece in range(PIECES):
        pass_x(c, None, piece)
    for t in range(2, n):
        hidden_step(t)
        if t == 2:
            for far in range(2, n):
                send_w(far, 1)
                send_w(far, -1)
            for slot, target, cond in routes():
                launch(
                    remote(
                        og_ref.at[:, cols(target, LANES)],
                        ogbuf.at[part(c, rows), :],
                        og_send.at[slot],
                        og_recv.at[c],
                        {"ctx": target},
                    ),
                    cond,
                )
        x_step(t - 1)
        w_step(t - 1)
        if t == 2:
            tables()
    x_step(n - 1)
    w_step(n - 1)
    for block in range(n):
        for column in range(wide):
            mine = (column // subs == h) & (column % subs == s)
            across = (column // subs != h) & (column % subs == s)

            @pl.when(jnp.logical_not(mine | across))
            def _():
                for piece in range(PIECES):
                    arrived(block, column, piece).wait_recv()

    for number, copy in enumerate(locals_):
        if number != 2:
            copy.wait()

    def gather_low(block, carry):
        here = part(block, rows)
        a_both = jnp.concatenate([aq_ref[...].astype(f32), av_ref[...].astype(f32)], axis=0).astype(bf16)
        lowbuf[here, :] = dot_t(hbuf[here, :], a_both).astype(bf16)
        return carry

    def multiply(slice_, fresh):
        deep = cols(slice_, depth)

        def rows_of(block, carry):
            here = part(block, rows)
            y = jnp.dot(hbuf[here, deep], wbuf[part(slice_, depth), :], preferred_element_type=f32)
            if fresh:
                acc[here, :] = y
            else:
                acc[here, :] += y
            return carry

        lax.fori_loop(0, n, rows_of, 0)

    lax.fori_loop(0, n, gather_low, 0)
    multiply(c, True)
    for t in range(1, n):
        for block, cond in ((c - t, c - t >= 0), (c + t, c + t < n)):

            @pl.when(cond)
            def _():
                for m in range(3):
                    remote(
                        wblk(block, m, 1 - r),
                        wblk(block, m, 1 - r),
                        wy_send.at[0, 0],
                        w_recv.at[block, m, 1 - r],
                        {"rep": 1 - r},
                    ).wait_recv()
                multiply(block, False)

    for block in range(n):

        @pl.when(block != c)
        def _():
            remote(
                ogbuf.at[part(block, rows), :], ogbuf.at[part(block, rows), :], og_send.at[0], og_recv.at[block], {"sub": 1 - s}
            ).wait_recv()

    def turn(u, cosine, sine):
        return u * cosine + pltpu.roll(u, LANES // 2, 1) * sine

    empty = jnp.zeros((8, LANES), f32)
    bq = jnp.concatenate([bq_ref[:, cols(c, LANES)].astype(f32), empty], axis=0).astype(bf16)
    bv = jnp.concatenate([empty, bv_ref[:, cols(c, LANES)].astype(f32)], axis=0).astype(bf16)

    def project(block, carry):
        here = part(block, rows)
        y = acc[here, :]
        low = lowbuf[here, :]
        cosine, sine = ctab[here, :], stab[here, :]
        pre_q = y[:, :LANES] + 2.0 * jnp.dot(low, bq, preferred_element_type=f32)
        qbuf[here, :] = turn(pre_q, cosine, sine).astype(bf16)
        kbuf[here, :] = turn(y[:, LANES : 2 * LANES], cosine, sine).astype(bf16)
        vbuf[here, :] = (
            y[:, 2 * LANES : 3 * LANES] + 2.0 * jnp.dot(low, bv, preferred_element_type=f32)
        ).astype(bf16)
        return carry

    lax.fori_loop(0, n, project, 0)

    shift = jnp.where(hs * n + c >= HEADS // 2, group // 2, 0)
    scale = 1.0 / math.sqrt(HEAD_DIM)
    hg = group // 2
    allowed = lax.broadcasted_iota(jnp.int32, (group, group), 0) >= lax.broadcasted_iota(
        jnp.int32, (group, group), 1
    )

    def attend(g, carry):
        first = pl.ds(pl.multiple_of(lax.rem(g * group + shift, tokens), 8), hg)
        second = pl.ds(pl.multiple_of(lax.rem(g * group + hg + shift, tokens), 8), hg)

        def take(ref):
            return jnp.concatenate([ref[first, :], ref[second, :]], axis=0)

        def put(ref, value):
            ref[first, :] = value[:hg]
            ref[second, :] = value[hg:]

        q, k, v, grad = take(qbuf), take(kbuf), take(vbuf), take(ogbuf)
        scores = jnp.where(allowed, dot_t(q, k) * scale, -jnp.inf)
        highest = jnp.max(scores, axis=-1, keepdims=True)
        expo = jnp.where(allowed, jnp.exp(scores - highest), 0.0)
        probs = expo / jnp.sum(expo, axis=-1, keepdims=True)
        probs_b = probs.astype(bf16)
        out = jnp.dot(probs_b, v, preferred_element_type=f32).astype(bf16)
        put(obuf, out)
        dprob = dot_t(grad, v)
        delta = jnp.sum(grad.astype(f32) * out.astype(f32), axis=-1, keepdims=True)
        dscore_b = (probs * (dprob - delta) * scale).astype(bf16)
        dq = jnp.dot(dscore_b, k, preferred_element_type=f32)
        put(dqbuf, turn(dq, take(ctab), -take(stab)).astype(bf16))
        put(dvbuf, t_dot(probs_b, grad).astype(bf16))
        return carry

    lax.fori_loop(0, tokens // group, attend, 0)

    dq, dv, low = dqbuf[...], dvbuf[...], lowbuf[...]
    low_t = 2.0 * (dot_t(bq, dq) + dot_t(bv, dv))
    for k in range(members):
        at = (k // 2) * LANES
        rsend[k] = low_t[8 * (k % 2) : 8 * (k % 2) + 8, at : at + LANES]
    for k in range(1, members):
        to = lax.rem(me + k, members)
        launch(remote(rsend.at[to], rrecv.at[me], rs_send.at[k], rs_recv.at[me], member(to)))
    gbsend[0:8, :] = (2.0 * t_dot(low, dq))[0:8]
    gbsend[8:16, :] = (2.0 * t_dot(low, dv))[8:16]
    for slot, target, cond in routes():
        launch(remote(gbsend, gbrecv.at[c], gb_send.at[slot], gb_recv.at[c], {"ctx": target}), cond)
    out_ref[:, cols(c, LANES)] = obuf[part(c, rows), :]
    gbq_ref[:, cols(c, LANES)] = gbsend[0:8, :]
    gbv_ref[:, cols(c, LANES)] = gbsend[8:16, :]

    rrecv[me] = rsend[me]
    for k in range(1, members):
        frm = lax.rem(me + k, members)
        remote(rsend.at[0], rrecv.at[frm], rs_send.at[0], rs_recv.at[frm], {"sub": 1 - s}).wait_recv()
    reduced = rrecv[0]
    for k in range(1, members):
        reduced = reduced + rrecv[k]
    total[...] = reduced
    agbuf[me] = reduced
    for k in range(1, members):
        to = lax.rem(me + k, members)
        launch(remote(total, agbuf.at[me], ag_send.at[k], ag_recv.at[me], member(to)))
    for slot, target, cond in routes():
        launch(
            remote(
                obuf.at[part(target, rows), :], outbuf.at[c], out_send.at[slot], out_recv.at[c], {"ctx": target}
            ),
            cond,
        )
    for k in range(1, members):
        frm = lax.rem(me + k, members)
        remote(total, agbuf.at[frm], ag_send.at[0], ag_recv.at[frm], {"sub": 1 - s}).wait_recv()
    full = jnp.concatenate(
        [
            jnp.concatenate([agbuf[2 * k + side] for k in range(members // 2)], axis=1)
            for side in range(2)
        ],
        axis=0,
    )
    upper = full.astype(bf16)
    lower = (full - upper.astype(f32)).astype(bf16)
    both = jnp.concatenate([upper, lower], axis=0)
    tile = 512

    def back(number, carry):
        here = pl.ds(pl.multiple_of(number * tile, LANES), tile)
        product = jnp.dot(both, hbuf[:, here], preferred_element_type=f32)
        gaq_ref[:, here] = product[0:8] + product[16:24]
        gav_ref[:, here] = product[8:16] + product[24:32]
        return carry

    lax.fori_loop(0, hbuf.shape[1] // tile, back, 0)
    for block in range(n):

        @pl.when(block != c)
        def _():
            remote(gbsend, gbrecv.at[block], gb_send.at[0], gb_recv.at[block], {"sub": 1 - s}).wait_recv()
            remote(outbuf.at[block], outbuf.at[block], out_send.at[0], out_recv.at[block], {"sub": 1 - s}).wait_recv()
            gbq_ref[:, block * LANES : (block + 1) * LANES] = gbrecv[block, 0:8, :]
            gbv_ref[:, block * LANES : (block + 1) * LANES] = gbrecv[block, 8:16, :]
            out_ref[:, block * LANES : (block + 1) * LANES] = outbuf[block]

    for copy, cond in pending:
        if cond is None:
            copy.wait_send()
        else:
            pl.when(cond)(copy.wait_send)


def one_head(
    hidden_states, w_query, w_key, w_value, a_query, a_value, b_query, b_value, positions, out_grad
):
    f32, bf16 = jnp.float32, jnp.bfloat16
    n, subs = lax.axis_size("ctx"), lax.axis_size("sub")
    wide = subs * lax.axis_size("head")
    rows, width = hidden_states.shape
    model = a_query.shape[0]
    rank = a_query.shape[1]
    tokens = rows * n
    columns = w_query.shape[1]
    members = n * wide
    pos = positions.reshape(rows // LANES, LANES)
    vmem, dma = pltpu.VMEM, pltpu.SemaphoreType.DMA
    hbm_spec = pl.BlockSpec(memory_space=pl.ANY)
    vmem_spec = pl.BlockSpec(memory_space=pltpu.VMEM)
    out, gaq, gbq, gav, gbv = pl.pallas_call(
        functools.partial(one_head_kernel, n, subs, wide),
        out_shape=(
            jax.ShapeDtypeStruct((rows, columns), bf16),
            jax.ShapeDtypeStruct((rank, model), f32),
            jax.ShapeDtypeStruct((rank, columns), f32),
            jax.ShapeDtypeStruct((rank, model), f32),
            jax.ShapeDtypeStruct((rank, columns), f32),
        ),
        in_specs=[hbm_spec] * 4 + [vmem_spec] * 4 + [hbm_spec] * 2,
        out_specs=[vmem_spec] * 5,
        scratch_shapes=[
            vmem((tokens, model), bf16),
            vmem((model, 3 * LANES), bf16),
            vmem((tokens, LANES), bf16),
            vmem((n, rows // LANES, LANES), jnp.int32),
            vmem((tokens, LANES), f32),
            vmem((tokens, LANES), f32),
            vmem((tokens, LANES), bf16),
            vmem((tokens, LANES), bf16),
            vmem((tokens, LANES), bf16),
            vmem((tokens, 3 * LANES), f32),
            vmem((tokens, 2 * rank), bf16),
            vmem((tokens, LANES), bf16),
            vmem((tokens, LANES), bf16),
            vmem((tokens, LANES), bf16),
            vmem((n, rows, LANES), bf16),
            vmem((2 * rank, LANES), f32),
            vmem((n, 2 * rank, LANES), f32),
            vmem((members, 8, LANES), f32),
            vmem((members, 8, LANES), f32),
            vmem((8, LANES), f32),
            vmem((members, 8, LANES), f32),
            dma((6,)),
            dma((2, n, PIECES)),
            dma((n, PIECES)),
            dma((2, n, PIECES)),
            dma((n, wide, PIECES)),
            dma((2 * n, 3)),
            dma((n, 3)),
            dma((n, 3, 2)),
            dma((2 * n,)),
            dma((n,)),
            dma((2 * n,)),
            dma((n,)),
            dma((2 * n,)),
            dma((n,)),
            dma((2 * n,)),
            dma((n,)),
            dma((members,)),
            dma((members,)),
            dma((members,)),
            dma((members,)),
        ],
        compiler_params=pltpu.CompilerParams(
            collective_id=0, has_side_effects=True, vmem_limit_bytes=56 * 1024 * 1024
        ),
    )(
        hidden_states, w_query, w_key, w_value, a_query.T, a_value.T, b_query, b_value, pos, out_grad
    )
    return (out, gaq.T, gbq, gav.T, gbv)


def fits_one_head(mesh, args):
    hidden_states, w_query, a_query = args[0], args[1], args[4]
    n = mesh.shape["ctx"]
    heads_here = w_query.shape[1] // HEAD_DIM
    rows = hidden_states.shape[0]
    members = n * mesh.shape["head"] * mesh.shape["sub"]
    return (
        mesh.shape["rep"] == 2
        and mesh.shape["head"] == 2
        and mesh.shape["sub"] == 2
        and heads_here == n
        and HEAD_DIM == LANES
        and a_query.shape[1] == 8
        and rows % LANES == 0
        and rows % (16 * PIECES) == 0
        and rows // LANES <= 8
        and 2 * rows * n // LANES == members
        and rows * n * a_query.shape[0] <= 2**22
    )


def choose(mesh, *args):
    return one_head(*args) if fits_one_head(mesh, args) else local(*args)


def solution(mesh):
    in_specs = (
        P(("rep", "ctx"), ("head", "sub")),
        P("ctx", ("head", "sub")),
        P("ctx", ("head", "sub")),
        P("ctx", ("head", "sub")),
        P(),
        P(),
        P(None, ("head", "sub")),
        P(None, ("head", "sub")),
        P(("rep", "ctx")),
        P(("rep", "ctx"), ("head", "sub")),
    )
    out_specs = (
        P(("rep", "ctx"), ("head", "sub")),
        P(None, "rep"),
        P("rep", ("head", "sub")),
        P(None, "rep"),
        P("rep", ("head", "sub")),
    )
    return jax.shard_map(
        functools.partial(choose, mesh), mesh=mesh, in_specs=in_specs, out_specs=out_specs, check_vma=False
    )
```
